128 devices in a mesh: row: 8 (over y, x_hi), col: 16 (over x_lo, z, core).
Axes of the slice: x: 4 (x_hi: 2, x_lo: 2; x = x_hi * 2 + x_lo), y: 4, z: 4, core: 2. Of those that a mesh axis runs over, the one named last changes fastest.
Arguments:
- affinity: bfloat16 [8, 16, 32, 256, 256], P('row', 'col'), may hold values from 9e-05 to 32.4
- block_rows: int32 [8, 16, 32], P('row', 'col'), may hold values from 0 to 7, as said below
- block_cols: int32 [8, 16, 32], P('row', 'col'), may hold values from 0 to 15
- block_count: int32 [8, 16], P('row', 'col'), may hold values from 8 to 32, as said below
- labels: float32 [32768, 1024], P(('row', 'col')), may hold values from 0 to 1
- labelled: int32 [32768], P(('row', 'col')), may hold values 0 or 1
Outputs:
- scores: float32 [32768, 1024], P(('row', 'col'))
The draws below stay inside these ranges and needn't reach their ends.
Inputs may be any that keep to these rules, and one draw needn't show every extreme that they name: Within one entry (r, c) the pairs (block_rows, block_cols) of all 32 slots are distinct, and its first 8 slots name every row block once. `block_count`: some entry has all 32 slots live.
All inputs are finite; a program needn't handle non-finite values. No bound on the sum of `labelled` on one device may be relied on, other than what follows from the above.
Results may differ from the reference program's by a relative error of at most 0.0003.
Values may be sent and summed in bfloat16 or wider, within the bound.
A program may use at most 128 MiB of HBM per device.

```python
import jax
import jax.numpy as jnp
from jax import lax

CLASSES = 1024
BS = 256
SWEEPS = 2
PROW = 8
PCOL = 16
MAXB = 32
NODES = 32768


def slot_layout(key):
    first_key, second_key = jax.random.split(jax.random.fold_in(key, 7))
    row_keys = jax.random.split(first_key, PROW * PCOL)
    row_perm = jax.vmap(lambda k: jax.random.permutation(k, PROW))(row_keys).reshape(PROW, PCOL, PROW)
    slot_index = jnp.arange(MAXB)
    local_row = slot_index % PROW
    slot_round = slot_index // PROW
    row_ids = jnp.take(row_perm, local_row, axis=2)
    col_keys = jax.random.split(second_key, PROW * PCOL * PROW)
    col_perm = jax.vmap(lambda k: jax.random.permutation(k, PCOL))(col_keys).reshape(PROW, PCOL, PROW, PCOL)
    picked = jnp.take_along_axis(col_perm, jnp.broadcast_to(row_ids[:, :, :, None], (PROW, PCOL, MAXB, 1)), axis=2)
    picked = picked.reshape(PROW, PCOL, MAXB, PCOL)
    round_index = jnp.broadcast_to(slot_round[None, None, :, None], (PROW, PCOL, MAXB, 1))
    col_ids = jnp.take_along_axis(picked, round_index, axis=3)[..., 0]
    return (row_ids.astype(jnp.int32), col_ids.astype(jnp.int32))


def cluster_total():
    return max(4, NODES // 512)


def node_clusters(key):
    return jax.random.randint(jax.random.fold_in(key, 13), (NODES,), 0, cluster_total()).astype(jnp.int32)


def draw_block_rows(key, part):
    return slot_layout(key)[0]


def draw_block_cols(key, part):
    return slot_layout(key)[1]


def draw_block_count(key, part):
    count_key, pick_key = jax.random.split(jax.random.fold_in(key, 11))
    counts = jax.random.randint(count_key, (PROW * PCOL,), PROW, MAXB + 1)
    chosen = jax.random.randint(pick_key, (), 0, PROW * PCOL)
    counts = jnp.where(jnp.arange(PROW * PCOL) == chosen, MAXB, counts)
    return counts.reshape(PROW, PCOL).astype(jnp.int32)


def draw_affinity(key, part):
    row_ids, col_ids = slot_layout(key)
    cluster_grid = node_clusters(key).reshape(PROW, PCOL, BS)
    grid_cols = jnp.broadcast_to(jnp.arange(PCOL)[None, :, None], row_ids.shape)
    grid_rows = jnp.broadcast_to(jnp.arange(PROW)[:, None, None], col_ids.shape)
    row_cluster = cluster_grid[row_ids, grid_cols]
    col_cluster = cluster_grid[grid_rows, col_ids]
    same = row_cluster[..., :, None] == col_cluster[..., None, :]
    mask_key, value_key = jax.random.split(jax.random.fold_in(key, 17), 2)
    pair_table = jax.random.uniform(jax.random.fold_in(key, 23), (cluster_total(), cluster_total()), jnp.float32)
    closeness = pair_table[row_cluster[..., :, None], col_cluster[..., None, :]]
    full_shape = (PROW, PCOL, MAXB, BS, BS)
    pick = jax.random.uniform(mask_key, full_shape, jnp.float32)
    level = jax.random.uniform(value_key, full_shape, jnp.float32)
    strong = same & (pick < 0.5)
    slot_factor = jnp.where(jnp.arange(MAXB) >= PROW, 4.0, 1.0).astype(jnp.float32)[None, None, :, None, None]
    floor_level = 0.5 * closeness + 0.5 * level
    floor_value = 0.0001 * jnp.exp(jnp.log(490.0) * floor_level)
    strong_value = jnp.exp(jnp.log(10.0) * (level - 1.0))
    values = jnp.where(strong, strong_value, floor_value)
    values = values * slot_factor
    return values.astype(jnp.float32).astype(jnp.bfloat16)


def draw_labels(key, part):
    cluster = node_clusters(key)
    profile_key, noise_key = jax.random.split(jax.random.fold_in(key, 19))
    profile = jax.random.uniform(profile_key, (cluster_total(), CLASSES), jnp.float32)
    noise = jax.random.uniform(noise_key, (NODES, CLASSES), jnp.float32)
    shared = jnp.take(profile, cluster, axis=0)
    values = 0.5 * noise + 0.5 * shared
    return values.astype(jnp.float32)


def place_ends(values, own_key, smallest, top_value):
    spot = [jax.random.randint(jax.random.fold_in(own_key, axis), (), 0, length) for axis, length in enumerate(values.shape)]
    longest = values.shape.index(max(values.shape))
    next_to = spot[:longest] + [(spot[longest] + 1) % values.shape[longest]] + spot[longest + 1:]
    return values.at[tuple(spot)].set(smallest).at[tuple(next_to)].set(top_value)


def setup_inputs(seed: int = 0) -> dict:
    keys = jax.random.split(jax.random.key(seed), 7)
    return {
        "affinity": draw_affinity(jax.random.fold_in(keys[6], 71), 0),
        "block_rows": draw_block_rows(jax.random.fold_in(keys[6], 71), 0),
        "block_cols": draw_block_cols(jax.random.fold_in(keys[6], 71), 0),
        "block_count": draw_block_count(jax.random.fold_in(keys[6], 71), 0),
        "labels": draw_labels(jax.random.fold_in(keys[6], 71), 0),
        "labelled": place_ends((jax.random.randint(keys[5], (NODES,), 0, 4) < 1).astype(jnp.int32), jax.random.fold_in(keys[5], 1), 0, 1),
    }


spread_weight = 0.8


def placement_table(row_ids, slot_live):
    return ((row_ids[None, :] == jnp.arange(PROW)[:, None]) & slot_live[None, :]).astype(jnp.float32)


def device_term(tile_stack, row_ids, col_ids, live_count, gathered):
    slot_live = jnp.arange(tile_stack.shape[0]) < live_count
    fetched = jnp.take(gathered, col_ids, axis=0).astype(jnp.float32)
    product = jnp.einsum("bij,bjc->bic", tile_stack.astype(jnp.float32), fetched, precision=lax.Precision.HIGHEST)
    placing = placement_table(row_ids, slot_live)
    return jnp.einsum("rb,bic->ric", placing, product, precision=lax.Precision.HIGHEST)


def reference(affinity, block_rows, block_cols, block_count, labels, labelled):
    label_grid = labels.reshape(PROW, PCOL, BS, CLASSES)
    keep_rows = labelled.reshape(PROW, PCOL, BS, 1) == 1

    def add_degree(flat, running):
        grid_row = flat // PCOL
        grid_col = flat % PCOL
        tile_stack = affinity[grid_row, grid_col]
        slot_live = jnp.arange(MAXB) < block_count[grid_row, grid_col]
        row_sums = jnp.sum(tile_stack.astype(jnp.float32), axis=2)
        placing = placement_table(block_rows[grid_row, grid_col], slot_live)
        part_sum = jnp.dot(placing, row_sums, precision=lax.Precision.HIGHEST)
        return running.at[:, grid_col].add(part_sum)

    degree = lax.fori_loop(0, PROW * PCOL, add_degree, jnp.zeros((PROW, PCOL, BS), jnp.float32))
    current = label_grid
    for iteration in range(SWEEPS):
        coarse = current.astype(jnp.bfloat16)

        def add_device(flat, running):
            grid_row = flat // PCOL
            grid_col = flat % PCOL
            gathered = lax.dynamic_index_in_dim(coarse, grid_row, 0, keepdims=False)
            term = device_term(affinity[grid_row, grid_col], block_rows[grid_row, grid_col],
                               block_cols[grid_row, grid_col], block_count[grid_row, grid_col], gathered)
            return running.at[:, grid_col].add(term)

        summed = lax.fori_loop(0, PROW * PCOL, add_device, jnp.zeros((PROW, PCOL, BS, CLASSES), jnp.float32))
        spread = spread_weight * summed / degree[..., None] + (1.0 - spread_weight) * label_grid
        current = jnp.where(keep_rows, label_grid, spread)
    return current.reshape(NODES, CLASSES)
```

```python
import jax
import jax.numpy as jnp
from jax import lax
from jax.experimental import pallas as pl
from jax.experimental.pallas import tpu as pltpu
from jax.sharding import PartitionSpec as P

MESH = pl.DeviceIdType.MESH
SWEEPS = 2
CHUNKS = 4
STRIP = 64
SPREAD = 0.8

PER_NAT = 2048.0 / 0.6931471805599453
ONE_CODE = 32700.0
LEAST = -32768.0


def encode(v):
    code = jnp.log(jnp.maximum(v, 1e-30)) * PER_NAT + ONE_CODE
    code = jnp.minimum(jnp.maximum(code, LEAST), 32767.0)
    return jnp.floor(code + 0.5).astype(jnp.int32).astype(jnp.int16)


def decode(q):
    code = q.astype(jnp.int32).astype(jnp.float32)
    v = jnp.exp((code - ONE_CODE) * (1.0 / PER_NAT))
    return jnp.where(code > LEAST, v, 0.0)


def make_kernel(sizes):
    slots, bs, classes, rows_n, cols_n = sizes
    width = classes // CHUNKS
    half = bs // 2
    steps = SWEEPS * CHUNKS

    def kernel(rows_s, cols_s, count_s, aff, labels, marked, out, wv, sums, deg_run, deg_all, inv, mask, prev_s, last_s,
               kept, *rest):
        xs = rest[:steps]
        outs = [rest[steps + 14 * q : steps + 14 * q + 7] for q in range(steps)]
        ins = [rest[steps + 14 * q + 7 : steps + 14 * q + 14] for q in range(steps)]
        (w_sem, xl_sem, z_sem, zr_sem, sib_sem, ag_send, rl_sem, nb_sem, xh_sem, rs_send, dg_recv, dg_send) = rest[15 * steps :]

        r, c = lax.axis_index("row"), lax.axis_index("col")
        y, xh = r // 2, r % 2
        xl, z, core = c // 8, (c // 2) % 4, c % 2
        zs = [(z + k) % 4 for k in range(4)]
        ys = [(y + k) % 4 for k in range(4)]
        col_of = lambda a, b, k: a * 8 + b * 2 + k
        sib = (r, col_of(xl, z, 1 - core))
        far_xl = (r, col_of(1 - xl, z, core))
        z_to = ((r, col_of(xl, zs[1], core)), (r, col_of(xl, zs[3], core)))
        y_to = ((ys[1] * 2 + xh, c), (ys[3] * 2 + xh, c))
        xh_to = (y * 2 + 1 - xh, c)
        rows_to = [((r + k) % rows_n, c) for k in range(1, rows_n)]

        barrier = pltpu.get_barrier_semaphore()
        met = [sib, far_xl, *z_to, *rows_to]
        for device in met:
            pl.semaphore_signal(barrier, inc=1, device_id=device, device_id_type=MESH)
        pl.semaphore_wait(barrier, len(met))

        def copy(src, dst, send, recv, device):
            return pltpu.make_async_remote_copy(
                src_ref=src, dst_ref=dst, send_sem=send, recv_sem=recv, device_id=device, device_id_type=MESH
            )

        def put(q, ref, recv, device):
            copy(ref, ref, ag_send.at[q], recv, device).start()

        def got(q, ref, recv, device):
            copy(ref, ref, ag_send.at[q], recv, device).wait_recv()

        def gather_own(q):
            own = xs[q].at[c]
            put(q, own, xl_sem.at[q], far_xl)
            put(q, own, z_sem.at[q, 0, 0], z_to[0])
            put(q, own, z_sem.at[q, 0, 1], z_to[1])
            put(q, own, sib_sem.at[q, 0], sib)

        def gather_pair(q):
            block = xs[q].at[col_of(1 - xl, z, core)]
            got(q, block, xl_sem.at[q], far_xl)
            put(q, block, z_sem.at[q, 1, 0], z_to[0])
            put(q, block, z_sem.at[q, 1, 1], z_to[1])
            put(q, block, sib_sem.at[q, 1], sib)

        def gather_near(q):
            for kind in (0, 1):
                side = xl if kind == 0 else 1 - xl
                for d in (0, 1):
                    b = col_of(side, zs[3] if d == 0 else zs[1], core)
                    got(q, xs[q].at[b], z_sem.at[q, kind, d], z_to[d])
                    put(q, xs[q].at[b, pl.ds(half * d, half)], zr_sem.at[q, kind, d], z_to[d])
                    put(q, xs[q].at[b], sib_sem.at[q, 2 + 2 * kind + d], sib)

        def gather_far(q):
            for kind in (0, 1):
                b = col_of(xl if kind == 0 else 1 - xl, zs[2], core)
                for d in (0, 1):
                    part = xs[q].at[b, pl.ds(half * d, half)]
                    got(q, part, zr_sem.at[q, kind, d], z_to[d])
                    put(q, part, sib_sem.at[q, 6 + 2 * kind + d], sib)

        def gather_sibling(q):
            for kind in (0, 1):
                side = xl if kind == 0 else 1 - xl
                got(q, xs[q].at[col_of(side, z, 1 - core)], sib_sem.at[q, kind], sib)
                for d in (0, 1):
                    near = xs[q].at[col_of(side, zs[3] if d == 0 else zs[1], 1 - core)]
                    got(q, near, sib_sem.at[q, 2 + 2 * kind + d], sib)
                    far = xs[q].at[col_of(side, zs[2], 1 - core), pl.ds(half * d, half)]
                    got(q, far, sib_sem.at[q, 6 + 2 * kind + d], sib)

        def products(q):
            def four(i, _):
                for k in range(4):
                    s = i * 4 + k
                    block = xs[q][cols_s[0, 0, s]]
                    sums[s + 1] = sums[prev_s[s]] + jnp.dot(wv[s], block, preferred_element_type=jnp.float32)
                return 0

            lax.fori_loop(0, slots // 4, four, 0)

        def share(rho, first):
            scale = inv[rho, pl.ds(first, STRIP), :]
            scale = jnp.concatenate([scale] * (width // 128), axis=1)
            return sums[last_s[rho], pl.ds(first, STRIP), :] * scale

        per_half = half // STRIP

        def strips(count, body):
            def step(i, _):
                body(i)
                return 0

            lax.fori_loop(0, count, step, 0)

        def send_unit(q, unit, recv, device):
            copy(outs[q][unit], ins[q][unit], rs_send.at[q, unit], recv, device).start()

        def got_unit(q, unit, recv, device):
            copy(outs[q][unit], ins[q][unit], rs_send.at[q, unit], recv, device).wait_recv()

        def sums_first(q):
            for h in (0, 1):
                def relay(i):
                    side, first = i // per_half, (i % per_half) * STRIP
                    value = share(ys[2] * 2 + side, h * half + first)
                    outs[q][h][pl.ds(i * STRIP, STRIP), :] = encode(value)

                strips(2 * per_half, relay)
                send_unit(q, h, rl_sem.at[q, h], y_to[h])
            for d in (0, 1):
                def straight(i):
                    side, first = i // per_half, (i % per_half) * STRIP
                    value = share((ys[1] if d == 0 else ys[3]) * 2 + side, (1 - d) * half + first)
                    outs[q][2 + 2 * d + 1 - d][pl.ds(i * STRIP, STRIP), :] = encode(value)

                strips(2 * per_half, straight)
                send_unit(q, 2 + 2 * d + 1 - d, nb_sem.at[q, d, 1 - d], y_to[d])

        def sums_relay(q):
            for d in (0, 1):
                got_unit(q, d, rl_sem.at[q, d], y_to[d])

                def joined(i):
                    side, first = i // per_half, (i % per_half) * STRIP
                    value = share((ys[1] if d == 0 else ys[3]) * 2 + side, d * half + first)
                    at = pl.ds(i * STRIP, STRIP)
                    outs[q][2 + 2 * d + d][at, :] = encode(value + decode(ins[q][d][at, :]))

                strips(2 * per_half, joined)
                send_unit(q, 2 + 2 * d + d, nb_sem.at[q, d, d], y_to[d])

        def in_y(q, side, h, first):
            at = pl.ds(side * half + first, STRIP)
            value = share(y * 2 + side, h * half + first) + decode(ins[q][2 + h][at, :])
            return value + decode(ins[q][4 + h][at, :])

        def sums_y(q):
            for h in (0, 1):
                for d in (0, 1):
                    got_unit(q, 2 + 2 * d + h, nb_sem.at[q, d, h], y_to[d])
            for h in (0, 1):
                def other(i):
                    outs[q][6][pl.ds(h * half + i * STRIP, STRIP), :] = encode(in_y(q, 1 - xh, h, i * STRIP))

                strips(per_half, other)
            send_unit(q, 6, xh_sem.at[q], xh_to)
            for h in (0, 1):
                def own(i):
                    kept[pl.ds(h * half + i * STRIP, STRIP), :] = in_y(q, xh, h, i * STRIP)

                strips(per_half, own)

        def sums_x(q):
            got_unit(q, 6, xh_sem.at[q], xh_to)
            lanes = pl.ds((q % CHUNKS) * width, width)

            def finish(i):
                at = pl.ds(i * STRIP, STRIP)
                total = kept[at, :] + decode(ins[q][6][at, :])
                prior = labels[at, lanes]
                keep = jnp.concatenate([mask[at, :]] * (width // 128), axis=1)
                value = jnp.where(keep == 1.0, prior, SPREAD * total + (1.0 - SPREAD) * prior)
                if q < steps - CHUNKS:
                    xs[q + CHUNKS][c, at, :] = value.astype(jnp.bfloat16)
                else:
                    out[at, lanes] = value

            strips(2 * per_half, finish)
            if q < steps - CHUNKS:
                gather_own(q + CHUNKS)

        load = pltpu.make_async_copy(aff.at[0, 0], wv, w_sem)
        load.start()

        def first_scores(q):
            def cast(i):
                at = pl.ds(i * STRIP, STRIP)
                xs[q][c, at, :] = labels[at, pl.ds(q * width, width)].astype(jnp.bfloat16)

            strips(bs // STRIP, cast)
            gather_own(q)

        first_scores(0)
        live = count_s[0, 0]

        def chain(s, lasts):
            row = rows_s[0, 0, s]
            before = jnp.int32(0)
            new = []
            for rho in range(rows_n):
                before = jnp.where(row == rho, lasts[rho], before)
                new.append(jnp.where((row == rho) & (s < live), s + 1, lasts[rho]))
            prev_s[s] = before
            return tuple(new)

        lasts = lax.fori_loop(0, slots, chain, (jnp.int32(0),) * rows_n)
        for rho in range(rows_n):
            last_s[rho] = lasts[rho]
        sums[0] = jnp.zeros((bs, width), jnp.float32)
        deg_run[0] = jnp.zeros((8, bs), jnp.float32)
        gather_pair(0)
        first_scores(1)

        load.wait()

        def row_sums(i, _):
            ones = jnp.ones((8, bs), jnp.bfloat16)
            for k in range(4):
                s = i * 4 + k
                part = lax.dot_general(ones, wv[s], (((1,), (1,)), ((), ())), preferred_element_type=jnp.float32)
                deg_run[s + 1] = deg_run[prev_s[s]] + part
            return 0

        lax.fori_loop(0, slots // 4, row_sums, 0)
        for rho in range(rows_n):
            deg_all[r, pl.ds(rho, 1), :] = deg_run[last_s[rho], pl.ds(0, 1), :]
        for k, device in enumerate(rows_to):
            copy(deg_all.at[r], deg_all.at[r], dg_send, dg_recv.at[k], device).start()

        def degrees():
            for k in range(1, rows_n):
                block = deg_all.at[(r + rows_n - k) % rows_n]
                copy(block, block, dg_send, dg_recv.at[k - 1], rows_to[k - 1]).wait_recv()
            degree = deg_all[0]
            for k in range(1, rows_n):
                degree = degree + deg_all[k]
            marks = jnp.broadcast_to(marked[...].astype(jnp.float32), (8, bs))
            stack = jnp.concatenate([1.0 / degree, marks, jnp.zeros((112, bs), jnp.float32)], axis=0)
            turned = jnp.transpose(stack)
            for rho in range(rows_n):
                inv[rho] = jnp.broadcast_to(turned[:, rho : rho + 1], (bs, 128))
            mask[...] = jnp.broadcast_to(turned[:, rows_n : rows_n + 1], (bs, 128))

        for q in range(steps):
            if q > 0:
                gather_pair(q)
                sums_relay(q - 1)
            gather_near(q)
            if q > 0:
                if q + 1 < CHUNKS:
                    first_scores(q + 1)
                sums_y(q - 1)
            gather_far(q)
            if q > 0:
                sums_x(q - 1)
            gather_sibling(q)
            products(q)
            if q == 0:
                degrees()
            sums_first(q)
        sums_relay(steps - 1)
        sums_y(steps - 1)
        sums_x(steps - 1)

        for q in range(steps):
            sent = xs[q].at[pl.ds(0, 15)]
            copy(sent, sent, ag_send.at[q], xl_sem.at[q], sib).wait_send()
            for unit in range(7):
                copy(outs[q][unit], ins[q][unit], rs_send.at[q, unit], xh_sem.at[q], xh_to).wait_send()
        copy(deg_all.at[pl.ds(0, rows_n - 1)], deg_all.at[pl.ds(0, rows_n - 1)], dg_send, dg_recv.at[0], rows_to[0]).wait_send()

    return kernel


def solution(mesh):
    rows_n, cols_n = mesh.shape["row"], mesh.shape["col"]

    def on_device(affinity, block_rows, block_cols, block_count, labels, labelled):
        slots, bs = affinity.shape[2], affinity.shape[3]
        classes = labels.shape[1]
        width = classes // CHUNKS
        half = bs // 2
        steps = SWEEPS * CHUNKS
        dma = pltpu.SemaphoreType.DMA
        scratch = [
            pltpu.VMEM((slots, bs, bs), jnp.bfloat16),
            pltpu.VMEM((slots + 1, bs, width), jnp.float32),
            pltpu.VMEM((slots + 1, 8, bs), jnp.float32),
            pltpu.VMEM((rows_n, rows_n, bs), jnp.float32),
            pltpu.VMEM((rows_n, bs, 128), jnp.float32),
            pltpu.VMEM((bs, 128), jnp.float32),
            pltpu.SMEM((slots,), jnp.int32),
            pltpu.SMEM((rows_n,), jnp.int32),
            pltpu.VMEM((bs, width), jnp.float32),
            *[pltpu.VMEM((cols_n, bs, width), jnp.bfloat16)] * steps,
            *[pltpu.VMEM((bs, width), jnp.int16)] * (14 * steps),
            dma,
            dma((steps,)),
            dma((steps, 2, 2)),
            dma((steps, 2, 2)),
            dma((steps, 10)),
            dma((steps,)),
            dma((steps, 2)),
            dma((steps, 2, 2)),
            dma((steps,)),
            dma((steps, 7)),
            dma((rows_n - 1,)),
            dma,
        ]
        smem = pl.BlockSpec(memory_space=pltpu.SMEM)
        vmem = pl.BlockSpec(memory_space=pltpu.VMEM)
        return pl.pallas_call(
            make_kernel((slots, bs, classes, rows_n, cols_n)),
            out_shape=jax.ShapeDtypeStruct(labels.shape, jnp.float32),
            in_specs=[smem, smem, smem, pl.BlockSpec(memory_space=pl.ANY), vmem, vmem],
            out_specs=vmem,
            scratch_shapes=scratch,
            compiler_params=pltpu.CompilerParams(
                collective_id=0, has_side_effects=True, vmem_limit_bytes=60 * 1024 * 1024
            ),
        )(block_rows, block_cols, block_count, affinity, labels, labelled.reshape(1, bs))

    placed = (
        P("row", "col", None, None, None),
        P("row", "col", None),
        P("row", "col", None),
        P("row", "col"),
        P(("row", "col"), None),
        P(("row", "col")),
    )
    return jax.shard_map(
        on_device, mesh=mesh, in_specs=placed, out_specs=P(("row", "col"), None), check_vma=False
    )
```

```python
import jax
import jax.numpy as jnp
from jax import lax
from jax.experimental import pallas as pl
from jax.experimental.pallas import tpu as pltpu
from jax.sharding import PartitionSpec as P

MESH = pl.DeviceIdType.MESH
SWEEPS = 2
WIDTHS = (256, 256, 256, 256)
PIECES = 2
STRIP = 64
SPREAD = 0.8

ORDER = (
    2000, 2010, 0, 3000, 4001, 4000, 4002, 4003, 4011, 4010, 1000, 5001, 5000, 3010, 2020, 5002, 5003, 6000,
    6001, 7000, 7001, 5011, 4013, 5010, 8001, 4012, 3020, 8000, 2030, 4021, 9000, 5013, 5012, 4020, 10000,
    10001, 6010, 6011, 7010, 7011, 4023, 4022, 3030, 4030, 11000, 8010, 5021, 9010, 8011, 5023, 5022, 4031,
    5020, 10010, 10011, 6020, 4032, 4033, 12000, 2040, 6021, 7020, 7021, 5033, 8021, 5030, 11010, 5032, 5031,
    9020, 8020, 3040, 6030, 4040, 4041, 10020, 10021, 6031, 12010, 2050, 4043, 7030, 8030, 4042, 5040, 5041,
    7031, 8031, 11020, 3050, 4051, 9030, 4050, 10030, 5042, 5043, 10031, 6040, 12020, 2060, 6041, 7040, 7041,
    4052, 4053, 8040, 11030, 9040, 5051, 8041, 5050, 4061, 4060, 5052, 5053, 3060, 10040, 10041, 6050, 12030,
    2070, 6051, 5061, 7050, 7051, 8051, 4062, 4063, 3070, 8050, 4071, 5060, 4070, 11040, 9050, 5063, 5062,
    10050, 10051, 6060, 4072, 4073, 6061, 7060, 7061, 9060, 5071, 5070, 8060, 8061, 5072, 5073, 6070, 10060,
    10061, 6071, 7071, 7070, 8070, 12040, 9070, 8071, 11050, 11060, 10070, 10071, 11070, 12060, 12050, 12070,
)

PER_NAT = 2048.0 / 0.6931471805599453
ONE_CODE = 32700.0
LEAST = -32768.0


def encode(v):
    code = jnp.log(jnp.maximum(v, 1e-30)) * PER_NAT + ONE_CODE
    code = jnp.minimum(jnp.maximum(code, LEAST), 32767.0)
    return jnp.floor(code + 0.5).astype(jnp.int32).astype(jnp.int16)


def decode(q):
    code = q.astype(jnp.int32).astype(jnp.float32)
    v = jnp.exp((code - ONE_CODE) * (1.0 / PER_NAT))
    return jnp.where(code > LEAST, v, 0.0)


def make_kernel(sizes):
    slots, bs, rows_n, cols_n = sizes
    chunks = len(WIDTHS)
    half = bs // 2
    steps = SWEEPS * chunks
    per_half = half // STRIP

    def kernel(rows_s, cols_s, count_s, aff, labels, marked, out, wv, sums, deg_run, deg_all, inv, mask, prev_s, last_s, *rest):
        xs = rest[:steps]
        pend = rest[steps : 2 * steps]
        outs = [rest[2 * steps + 14 * q : 2 * steps + 14 * q + 7] for q in range(steps)]
        ins = [rest[2 * steps + 14 * q + 7 : 2 * steps + 14 * q + 14] for q in range(steps)]
        (w_sem, xl_sem, z_sem, zr_sem, sib_sem, ag_send, rl_sem, nb_sem, xh_sem, rs_send, dg_recv, dg_send) = rest[16 * steps :]

        r, c = lax.axis_index("row"), lax.axis_index("col")
        y, xh = r // 2, r % 2
        xl, z, core = c // 8, (c // 2) % 4, c % 2
        zs = [(z + k) % 4 for k in range(4)]
        ys = [(y + k) % 4 for k in range(4)]
        col_of = lambda a, b, k: a * 8 + b * 2 + k
        sib = (r, col_of(xl, z, 1 - core))
        far_xl = (r, col_of(1 - xl, z, core))
        z_to = ((r, col_of(xl, zs[1], core)), (r, col_of(xl, zs[3], core)))
        y_to = ((ys[1] * 2 + xh, c), (ys[3] * 2 + xh, c))
        xh_to = (y * 2 + 1 - xh, c)
        rows_to = [((r + k) % rows_n, c) for k in range(1, rows_n)]

        barrier = pltpu.get_barrier_semaphore()
        met = [sib, far_xl, *z_to, *rows_to]
        for device in met:
            pl.semaphore_signal(barrier, inc=1, device_id=device, device_id_type=MESH)
        load = pltpu.make_async_copy(aff.at[0, 0], wv, w_sem)
        load.start()
        pl.semaphore_wait(barrier, len(met))

        def width(q):
            return WIDTHS[q % chunks]

        def lanes(q):
            return pl.ds(sum(WIDTHS[: q % chunks]), width(q))

        def copy(src, dst, send, recv, device):
            return pltpu.make_async_remote_copy(
                src_ref=src, dst_ref=dst, send_sem=send, recv_sem=recv, device_id=device, device_id_type=MESH
            )

        def strips(count, body):
            def step(i, _):
                body(i)
                return 0

            lax.fori_loop(0, count, step, 0)

        def put(q, ref, recv, device):
            copy(ref, ref, ag_send.at[q], recv, device).start()

        def got(q, ref, recv, device):
            copy(ref, ref, ag_send.at[q], recv, device).wait_recv()

        def own(q):
            if q < chunks:
                def cast(i):
                    at = pl.ds(i * STRIP, STRIP)
                    xs[q][c, at, :] = labels[at, lanes(q)].astype(jnp.bfloat16)

                strips(bs // STRIP, cast)
            block = xs[q].at[c]
            put(q, block, xl_sem.at[q], far_xl)
            put(q, block, z_sem.at[q, 0, 0], z_to[0])
            put(q, block, z_sem.at[q, 0, 1], z_to[1])
            put(q, block, sib_sem.at[q, 0], sib)

        def pair(q):
            block = xs[q].at[col_of(1 - xl, z, core)]
            got(q, block, xl_sem.at[q], far_xl)
            put(q, block, z_sem.at[q, 1, 0], z_to[0])
            put(q, block, z_sem.at[q, 1, 1], z_to[1])
            put(q, block, sib_sem.at[q, 1], sib)

        def near(q, kind, d):
            b = col_of(xl if kind == 0 else 1 - xl, zs[3] if d == 0 else zs[1], core)
            got(q, xs[q].at[b], z_sem.at[q, kind, d], z_to[d])
            put(q, xs[q].at[b, pl.ds(half * d, half)], zr_sem.at[q, kind, d], z_to[d])
            put(q, xs[q].at[b], sib_sem.at[q, 2 + 2 * kind + d], sib)

        def far(q, kind, d):
            b = col_of(xl if kind == 0 else 1 - xl, zs[2], core)
            part = xs[q].at[b, pl.ds(half * d, half)]
            got(q, part, zr_sem.at[q, kind, d], z_to[d])
            put(q, part, sib_sem.at[q, 6 + 2 * kind + d], sib)

        def from_sibling(q):
            for kind in (0, 1):
                side = xl if kind == 0 else 1 - xl
                got(q, xs[q].at[col_of(side, z, 1 - core)], sib_sem.at[q, kind], sib)
                for d in (0, 1):
                    block = xs[q].at[col_of(side, zs[3] if d == 0 else zs[1], 1 - core)]
                    got(q, block, sib_sem.at[q, 2 + 2 * kind + d], sib)
                    part = xs[q].at[col_of(side, zs[2], 1 - core), pl.ds(half * d, half)]
                    got(q, part, sib_sem.at[q, 6 + 2 * kind + d], sib)

        def prod(q, piece):
            if piece == 0:
                from_sibling(q)
            wide = pl.ds(0, width(q))
            first = piece * (slots // PIECES)

            def four(i, _):
                for k in range(4):
                    s = first + i * 4 + k
                    block = xs[q][cols_s[0, 0, s]]
                    sums[s + 1, :, wide] = sums[prev_s[s], :, wide] + jnp.dot(wv[s], block, preferred_element_type=jnp.float32)
                return 0

            lax.fori_loop(0, slots // PIECES // 4, four, 0)

        def share(q, rho, first):
            scale = inv[rho, pl.ds(first, STRIP), :]
            scale = jnp.concatenate([scale] * (width(q) // 128), axis=1)
            return sums[last_s[rho], pl.ds(first, STRIP), pl.ds(0, width(q))] * scale

        def send_unit(q, unit, recv, device):
            copy(outs[q][unit], ins[q][unit], rs_send.at[q, unit], recv, device).start()

        def got_unit(q, unit, recv, device):
            copy(outs[q][unit], ins[q][unit], rs_send.at[q, unit], recv, device).wait_recv()

        def send_far(q, h):
            def relay(i):
                side, first = i // per_half, (i % per_half) * STRIP
                outs[q][h][pl.ds(i * STRIP, STRIP), :] = encode(share(q, ys[2] * 2 + side, h * half + first))

            strips(2 * per_half, relay)
            send_unit(q, h, rl_sem.at[q, h], y_to[h])

        def send_near(q, d):
            unit = 3 if d == 0 else 4

            def straight(i):
                side, first = i // per_half, (i % per_half) * STRIP
                value = share(q, (ys[1] if d == 0 else ys[3]) * 2 + side, (1 - d) * half + first)
                outs[q][unit][pl.ds(i * STRIP, STRIP), :] = encode(value)

            strips(2 * per_half, straight)
            send_unit(q, unit, nb_sem.at[q, d, 1 - d], y_to[d])

        def set_aside(q):
            for d in (0, 1):
                def wait_relay(i):
                    side, first = i // per_half, (i % per_half) * STRIP
                    value = share(q, (ys[1] if d == 0 else ys[3]) * 2 + side, d * half + first)
                    pend[q][pl.ds(d * bs + i * STRIP, STRIP), :] = value

                strips(2 * per_half, wait_relay)
            for side in (0, 1):
                def stay(i):
                    pend[q][pl.ds((2 + side) * bs + i * STRIP, STRIP), :] = share(q, y * 2 + side, i * STRIP)

                strips(2 * per_half, stay)

        def relay_on(q, d):
            unit = 2 if d == 0 else 5
            got_unit(q, d, rl_sem.at[q, d], y_to[d])

            def joined(i):
                at = pl.ds(i * STRIP, STRIP)
                value = pend[q][pl.ds(d * bs + i * STRIP, STRIP), :] + decode(ins[q][d][at, :])
                outs[q][unit][at, :] = encode(value)

            strips(2 * per_half, joined)
            send_unit(q, unit, nb_sem.at[q, d, d], y_to[d])

        def in_y(q, side, h, first):
            at = pl.ds(side * half + first, STRIP)
            value = pend[q][pl.ds((2 + side) * bs + h * half + first, STRIP), :] + decode(ins[q][2 + h][at, :])
            return value + decode(ins[q][4 + h][at, :])

        def over_y(q):
            for h in (0, 1):
                for d in (0, 1):
                    got_unit(q, 2 + 2 * d + h, nb_sem.at[q, d, h], y_to[d])
            for h in (0, 1):
                def other(i):
                    outs[q][6][pl.ds(h * half + i * STRIP, STRIP), :] = encode(in_y(q, 1 - xh, h, i * STRIP))

                strips(per_half, other)
            send_unit(q, 6, xh_sem.at[q], xh_to)
            for h in (0, 1):
                def mine(i):
                    value = in_y(q, xh, h, i * STRIP)
                    pend[q][pl.ds((2 + xh) * bs + h * half + i * STRIP, STRIP), :] = value

                strips(per_half, mine)

        def finish(q):
            got_unit(q, 6, xh_sem.at[q], xh_to)

            def update(i):
                at = pl.ds(i * STRIP, STRIP)
                total = pend[q][pl.ds((2 + xh) * bs + i * STRIP, STRIP), :] + decode(ins[q][6][at, :])
                prior = labels[at, lanes(q)]
                keep = jnp.concatenate([mask[at, :]] * (width(q) // 128), axis=1)
                value = jnp.where(keep == 1.0, prior, SPREAD * total + (1.0 - SPREAD) * prior)
                if q < steps - chunks:
                    xs[q + chunks][c, at, :] = value.astype(jnp.bfloat16)
                else:
                    out[at, lanes(q)] = value

            strips(2 * per_half, update)

        def degrees_out(q):
            live = count_s[0, 0]

            def chain(s, lasts):
                row = rows_s[0, 0, s]
                before = jnp.int32(0)
                new = []
                for rho in range(rows_n):
                    before = jnp.where(row == rho, lasts[rho], before)
                    new.append(jnp.where((row == rho) & (s < live), s + 1, lasts[rho]))
                prev_s[s] = before
                return tuple(new)

            lasts = lax.fori_loop(0, slots, chain, (jnp.int32(0),) * rows_n)
            for rho in range(rows_n):
                last_s[rho] = lasts[rho]
            sums[0] = jnp.zeros((bs, max(WIDTHS)), jnp.float32)
            deg_run[0] = jnp.zeros((8, bs), jnp.float32)
            load.wait()

            def row_sums(i, _):
                ones = jnp.ones((8, bs), jnp.bfloat16)
                for k in range(4):
                    s = i * 4 + k
                    part = lax.dot_general(ones, wv[s], (((1,), (1,)), ((), ())), preferred_element_type=jnp.float32)
                    deg_run[s + 1] = deg_run[prev_s[s]] + part
                return 0

            lax.fori_loop(0, slots // 4, row_sums, 0)
            for rho in range(rows_n):
                deg_all[r, pl.ds(rho, 1), :] = deg_run[last_s[rho], pl.ds(0, 1), :]
            for k, device in enumerate(rows_to):
                copy(deg_all.at[r], deg_all.at[r], dg_send, dg_recv.at[k], device).start()

        def degrees_in(q):
            for k in range(1, rows_n):
                block = deg_all.at[(r + rows_n - k) % rows_n]
                copy(block, block, dg_send, dg_recv.at[k - 1], rows_to[k - 1]).wait_recv()
            degree = deg_all[0]
            for k in range(1, rows_n):
                degree = degree + deg_all[k]
            marks = jnp.broadcast_to(marked[...].astype(jnp.float32), (8, bs))
            stack = jnp.concatenate([1.0 / degree, marks, jnp.zeros((112, bs), jnp.float32)], axis=0)
            turned = jnp.transpose(stack)
            for rho in range(rows_n):
                inv[rho] = jnp.broadcast_to(turned[:, rho : rho + 1], (bs, 128))
            mask[...] = jnp.broadcast_to(turned[:, rows_n : rows_n + 1], (bs, 128))

        phases = (degrees_out, degrees_in, own, pair, near, far, prod, send_far, send_near, set_aside, relay_on, over_y, finish)
        for code in ORDER:
            kind, q, more = code // 1000, code // 10 % 100, code % 10
            if kind in (4, 5):
                phases[kind](q, more // 2, more % 2)
            elif kind in (6, 7, 8, 10):
                phases[kind](q, more)
            else:
                phases[kind](q)

        for q in range(steps):
            sent = xs[q].at[pl.ds(0, 15)]
            copy(sent, sent, ag_send.at[q], xl_sem.at[q], sib).wait_send()
            for unit in range(7):
                copy(outs[q][unit], ins[q][unit], rs_send.at[q, unit], xh_sem.at[q], xh_to).wait_send()
        copy(deg_all.at[pl.ds(0, rows_n - 1)], deg_all.at[pl.ds(0, rows_n - 1)], dg_send, dg_recv.at[0], rows_to[0]).wait_send()

    return kernel


def solution(mesh):
    rows_n, cols_n = mesh.shape["row"], mesh.shape["col"]

    def on_device(affinity, block_rows, block_cols, block_count, labels, labelled):
        slots, bs = affinity.shape[2], affinity.shape[3]
        steps = SWEEPS * len(WIDTHS)
        each = WIDTHS * SWEEPS
        dma = pltpu.SemaphoreType.DMA
        scratch = [
            pltpu.VMEM((slots, bs, bs), jnp.bfloat16),
            pltpu.VMEM((slots + 1, bs, max(WIDTHS)), jnp.float32),
            pltpu.VMEM((slots + 1, 8, bs), jnp.float32),
            pltpu.VMEM((rows_n, rows_n, bs), jnp.float32),
            pltpu.VMEM((rows_n, bs, 128), jnp.float32),
            pltpu.VMEM((bs, 128), jnp.float32),
            pltpu.SMEM((slots,), jnp.int32),
            pltpu.SMEM((rows_n,), jnp.int32),
            *[pltpu.VMEM((cols_n, bs, width), jnp.bfloat16) for width in each],
            *[pltpu.VMEM((4 * bs, width), jnp.float32) for width in each],
            *[pltpu.VMEM((bs, width), jnp.int16) for width in each for _ in range(14)],
            dma,
            dma((steps,)),
            dma((steps, 2, 2)),
            dma((steps, 2, 2)),
            dma((steps, 10)),
            dma((steps,)),
            dma((steps, 2)),
            dma((steps, 2, 2)),
            dma((steps,)),
            dma((steps, 7)),
            dma((rows_n - 1,)),
            dma,
        ]
        smem = pl.BlockSpec(memory_space=pltpu.SMEM)
        vmem = pl.BlockSpec(memory_space=pltpu.VMEM)
        return pl.pallas_call(
            make_kernel((slots, bs, rows_n, cols_n)),
            out_shape=jax.ShapeDtypeStruct(labels.shape, jnp.float32),
            in_specs=[smem, smem, smem, pl.BlockSpec(memory_space=pl.ANY), vmem, vmem],
            out_specs=vmem,
            scratch_shapes=scratch,
            compiler_params=pltpu.CompilerParams(
                collective_id=0, has_side_effects=True, vmem_limit_bytes=60 * 1024 * 1024
            ),
        )(block_rows, block_cols, block_count, affinity, labels, labelled.reshape(1, bs))

    placed = (
        P("row", "col", None, None, None),
        P("row", "col", None),
        P("row", "col", None),
        P("row", "col"),
        P(("row", "col"), None),
        P(("row", "col")),
    )
    return jax.shard_map(
        on_device, mesh=mesh, in_specs=placed, out_specs=P(("row", "col"), None), check_vma=False
    )
```

```python
import jax
import jax.numpy as jnp
from jax import lax
from jax.experimental import pallas as pl
from jax.experimental.pallas import tpu as pltpu
from jax.sharding import PartitionSpec as P

MESH = pl.DeviceIdType.MESH
SWEEPS = 2
WIDTHS = (256, 256, 256, 256)
PIECES = 2
UNROLL = 8
SPREAD = 0.8

ORDER = (
    2000, 2010, 0, 3000, 4000, 4001, 4002, 4003, 1000, 3010, 4010, 5000, 4011, 5001, 5002, 5003, 2020, 6000,
    6001, 7000, 4012, 7002, 7001, 9000, 7003, 4013, 8002, 5011, 8000, 3020, 2030, 5010, 10000, 10002, 8003,
    4021, 8001, 5012, 5013, 10001, 4020, 10003, 6010, 6011, 11000, 7012, 7010, 7013, 4023, 7011, 4022, 9010,
    4030, 11001, 4031, 8012, 8010, 3030, 5021, 10010, 10012, 5022, 8013, 5020, 8011, 5023, 10013, 10011,
    12000, 2040, 6020, 6021, 7020, 7022, 11010, 7021, 4032, 4033, 8020, 7023, 5030, 11011, 5031, 3040, 8022,
    9020, 4041, 10022, 10020, 8021, 5033, 10023, 5032, 4040, 10021, 8023, 12010, 2050, 6030, 6031, 11020,
    7030, 7032, 7033, 4043, 7031, 5040, 4042, 8031, 9030, 11021, 3050, 8032, 4050, 5041, 10030, 10032, 8033,
    8030, 4051, 5043, 5042, 10031, 10033, 12020, 2060, 6040, 6041, 7042, 7040, 4053, 4052, 11030, 7043, 7041,
    8041, 9040, 3060, 8042, 11031, 5050, 8040, 4061, 8043, 5051, 4060, 10040, 10042, 5052, 5053, 10043, 10041,
    6050, 12030, 2070, 6051, 7051, 7053, 4062, 5060, 7052, 9050, 7050, 5061, 4063, 11040, 8050, 8053, 8051,
    8052, 3070, 5063, 5062, 4071, 4070, 10050, 10051, 10052, 10053, 6060, 6061, 4072, 4073, 7060, 7062, 7063,
    8062, 7061, 8061, 11041, 8060, 9060, 8063, 5071, 5070, 5072, 5073, 10060, 10062, 11050, 6070, 6071, 7070,
    7072, 8072, 12040, 9070, 10061, 8070, 10070, 10072, 11060, 7073, 10063, 7071, 8073, 11051, 11070, 8071,
    10073, 10071, 12050, 11061, 12060, 11071, 12070,
)

PER_NAT = 2048.0 / 0.6931471805599453
ONE_CODE = 32700.0
LEAST = -32768.0


def encode(v):
    code = jnp.log(jnp.maximum(v, 1e-30)) * PER_NAT + ONE_CODE
    code = jnp.minimum(jnp.maximum(code, LEAST), 32767.0)
    return jnp.floor(code + 0.5).astype(jnp.int32).astype(jnp.int16)


def decode(q):
    code = q.astype(jnp.int32).astype(jnp.float32)
    v = jnp.exp((code - ONE_CODE) * (1.0 / PER_NAT))
    return jnp.where(code > LEAST, v, 0.0)


def make_kernel(sizes):
    slots, bs, rows_n, cols_n = sizes
    chunks = len(WIDTHS)
    half = bs // 2
    steps = SWEEPS * chunks

    def kernel(rows_s, cols_s, count_s, aff, labels, marked, out, wv, sums, deg_run, deg_all, inv, mask, prev_s, last_s, *rest):
        xs = rest[:steps]
        pend = rest[steps : 2 * steps]
        outs = [rest[2 * steps + 26 * q : 2 * steps + 26 * q + 13] for q in range(steps)]
        ins = [rest[2 * steps + 26 * q + 13 : 2 * steps + 26 * q + 26] for q in range(steps)]
        (w_sem, xl_sem, z_sem, zr_sem, sib_sem, ag_send, rs_recv, rs_send, dg_recv, dg_send) = rest[28 * steps :]

        r, c = lax.axis_index("row"), lax.axis_index("col")
        y, xh = r // 2, r % 2
        xl, z, core = c // 8, (c // 2) % 4, c % 2
        zs = [(z + k) % 4 for k in range(4)]
        ys = [(y + k) % 4 for k in range(4)]
        col_of = lambda a, b, k: a * 8 + b * 2 + k
        sib = (r, col_of(xl, z, 1 - core))
        far_xl = (r, col_of(1 - xl, z, core))
        z_to = ((r, col_of(xl, zs[1], core)), (r, col_of(xl, zs[3], core)))
        y_to = ((ys[1] * 2 + xh, c), (ys[3] * 2 + xh, c))
        xh_to = (y * 2 + 1 - xh, c)
        sides = (1 - xh, xh)
        rows_to = [((r + k) % rows_n, c) for k in range(1, rows_n)]

        barrier = pltpu.get_barrier_semaphore()
        met = [sib, far_xl, *z_to, *rows_to]
        for device in met:
            pl.semaphore_signal(barrier, inc=1, device_id=device, device_id_type=MESH)
        load = pltpu.make_async_copy(aff.at[0, 0], wv, w_sem)
        load.start()
        pl.semaphore_wait(barrier, len(met))

        def width(q):
            return WIDTHS[q % chunks]

        def lanes(q):
            return pl.ds(sum(WIDTHS[: q % chunks]), width(q))

        def copy(src, dst, send, recv, device):
            return pltpu.make_async_remote_copy(
                src_ref=src, dst_ref=dst, send_sem=send, recv_sem=recv, device_id=device, device_id_type=MESH
            )

        def put(q, ref, recv, device):
            copy(ref, ref, ag_send.at[q], recv, device).start()

        def got(q, ref, recv, device):
            copy(ref, ref, ag_send.at[q], recv, device).wait_recv()

        def own(q):
            if q < chunks:
                for h in (0, 1):
                    at = pl.ds(h * half, half)
                    xs[q][c, at, :] = labels[at, lanes(q)].astype(jnp.bfloat16)
            block = xs[q].at[c]
            put(q, block, xl_sem.at[q], far_xl)
            put(q, block, z_sem.at[q, 0, 0], z_to[0])
            put(q, block, z_sem.at[q, 0, 1], z_to[1])
            put(q, block, sib_sem.at[q, 0], sib)

        def pair(q):
            block = xs[q].at[col_of(1 - xl, z, core)]
            got(q, block, xl_sem.at[q], far_xl)
            put(q, block, z_sem.at[q, 1, 0], z_to[0])
            put(q, block, z_sem.at[q, 1, 1], z_to[1])
            put(q, block, sib_sem.at[q, 1], sib)

        def near(q, kind, d):
            b = col_of(xl if kind == 0 else 1 - xl, zs[3] if d == 0 else zs[1], core)
            got(q, xs[q].at[b], z_sem.at[q, kind, d], z_to[d])
            put(q, xs[q].at[b, pl.ds(half * d, half)], zr_sem.at[q, kind, d], z_to[d])
            put(q, xs[q].at[b], sib_sem.at[q, 2 + 2 * kind + d], sib)

        def far(q, kind, d):
            b = col_of(xl if kind == 0 else 1 - xl, zs[2], core)
            part = xs[q].at[b, pl.ds(half * d, half)]
            got(q, part, zr_sem.at[q, kind, d], z_to[d])
            put(q, part, sib_sem.at[q, 6 + 2 * kind + d], sib)

        def from_sibling(q):
            for kind in (0, 1):
                side = xl if kind == 0 else 1 - xl
                got(q, xs[q].at[col_of(side, z, 1 - core)], sib_sem.at[q, kind], sib)
                for d in (0, 1):
                    block = xs[q].at[col_of(side, zs[3] if d == 0 else zs[1], 1 - core)]
                    got(q, block, sib_sem.at[q, 2 + 2 * kind + d], sib)
                    part = xs[q].at[col_of(side, zs[2], 1 - core), pl.ds(half * d, half)]
                    got(q, part, sib_sem.at[q, 6 + 2 * kind + d], sib)

        def prod(q, piece):
            if piece == 0:
                from_sibling(q)
            wide = pl.ds(0, width(q))
            first = piece * (slots // PIECES)

            def several(i, _):
                for k in range(UNROLL):
                    s = first + i * UNROLL + k
                    block = xs[q][cols_s[0, 0, s]]
                    sums[s + 1, :, wide] = sums[prev_s[s], :, wide] + jnp.dot(wv[s], block, preferred_element_type=jnp.float32)
                return 0

            lax.fori_loop(0, slots // PIECES // UNROLL, several, 0)

        def share(q, rho, h):
            at = pl.ds(h * half, half)
            scale = jnp.concatenate([inv[rho, at, :]] * (width(q) // 128), axis=1)
            return sums[last_s[rho], at, pl.ds(0, width(q))] * scale

        def send_unit(q, unit, device):
            copy(outs[q][unit], ins[q][unit], rs_send.at[q, unit], rs_recv.at[q, unit], device).start()

        def got_unit(q, unit, device):
            copy(outs[q][unit], ins[q][unit], rs_send.at[q, unit], rs_recv.at[q, unit], device).wait_recv()

        def next_y(d, o):
            return (ys[1] if d == 0 else ys[3]) * 2 + sides[o]

        def send_far(q, h, o):
            unit = 2 * h + o
            outs[q][unit][...] = encode(share(q, ys[2] * 2 + sides[o], h))
            send_unit(q, unit, y_to[h])

        def send_near(q, d, o):
            unit = 4 + 4 * d + 2 * (1 - d) + o
            outs[q][unit][...] = encode(share(q, next_y(d, o), 1 - d))
            send_unit(q, unit, y_to[d])

        def set_aside(q):
            for o in (0, 1):
                for d in (0, 1):
                    pend[q][pl.ds((2 * d + o) * half, half), :] = share(q, next_y(d, o), d)
                for h in (0, 1):
                    pend[q][pl.ds((4 + 2 * o + h) * half, half), :] = share(q, y * 2 + sides[o], h)

        def relay_on(q, d, o):
            unit = 4 + 4 * d + 2 * d + o
            got_unit(q, 2 * d + o, y_to[d])
            value = pend[q][pl.ds((2 * d + o) * half, half), :] + decode(ins[q][2 * d + o][...])
            outs[q][unit][...] = encode(value)
            send_unit(q, unit, y_to[d])

        def over_y(q, o):
            for h in (0, 1):
                for d in (0, 1):
                    got_unit(q, 4 + 4 * d + 2 * h + o, y_to[d])
            for h in (0, 1):
                at = pl.ds((4 + 2 * o + h) * half, half)
                value = pend[q][at, :] + decode(ins[q][4 + 2 * h + o][...]) + decode(ins[q][8 + 2 * h + o][...])
                if o == 0:
                    outs[q][12][pl.ds(h * half, half), :] = encode(value)
                else:
                    pend[q][at, :] = value
            if o == 0:
                send_unit(q, 12, xh_to)

        def finish(q):
            got_unit(q, 12, xh_to)
            for h in (0, 1):
                at = pl.ds(h * half, half)
                total = pend[q][pl.ds((6 + h) * half, half), :] + decode(ins[q][12][at, :])
                prior = labels[at, lanes(q)]
                keep = jnp.concatenate([mask[at, :]] * (width(q) // 128), axis=1)
                value = jnp.where(keep == 1.0, prior, SPREAD * total + (1.0 - SPREAD) * prior)
                if q < steps - chunks:
                    xs[q + chunks][c, at, :] = value.astype(jnp.bfloat16)
                else:
                    out[at, lanes(q)] = value

        def degrees_out(q):
            live = count_s[0, 0]

            def chain(s, lasts):
                row = rows_s[0, 0, s]
                before = jnp.int32(0)
                new = []
                for rho in range(rows_n):
                    before = jnp.where(row == rho, lasts[rho], before)
                    new.append(jnp.where((row == rho) & (s < live), s + 1, lasts[rho]))
                prev_s[s] = before
                return tuple(new)

            lasts = lax.fori_loop(0, slots, chain, (jnp.int32(0),) * rows_n)
            for rho in range(rows_n):
                last_s[rho] = lasts[rho]
            sums[0] = jnp.zeros((bs, max(WIDTHS)), jnp.float32)
            deg_run[0] = jnp.zeros((8, bs), jnp.float32)
            load.wait()

            def row_sums(i, _):
                ones = jnp.ones((8, bs), jnp.bfloat16)
                for k in range(4):
                    s = i * 4 + k
                    part = lax.dot_general(ones, wv[s], (((1,), (1,)), ((), ())), preferred_element_type=jnp.float32)
                    deg_run[s + 1] = deg_run[prev_s[s]] + part
                return 0

            lax.fori_loop(0, slots // 4, row_sums, 0)
            for rho in range(rows_n):
                deg_all[r, pl.ds(rho, 1), :] = deg_run[last_s[rho], pl.ds(0, 1), :]
            for k, device in enumerate(rows_to):
                copy(deg_all.at[r], deg_all.at[r], dg_send, dg_recv.at[k], device).start()

        def degrees_in(q):
            for k in range(1, rows_n):
                block = deg_all.at[(r + rows_n - k) % rows_n]
                copy(block, block, dg_send, dg_recv.at[k - 1], rows_to[k - 1]).wait_recv()
            degree = deg_all[0]
            for k in range(1, rows_n):
                degree = degree + deg_all[k]
            marks = jnp.broadcast_to(marked[...].astype(jnp.float32), (8, bs))
            stack = jnp.concatenate([1.0 / degree, marks, jnp.zeros((112, bs), jnp.float32)], axis=0)
            turned = jnp.transpose(stack)
            for rho in range(rows_n):
                inv[rho] = jnp.broadcast_to(turned[:, rho : rho + 1], (bs, 128))
            mask[...] = jnp.broadcast_to(turned[:, rows_n : rows_n + 1], (bs, 128))

        phases = (degrees_out, degrees_in, own, pair, near, far, prod, send_far, send_near, set_aside, relay_on, over_y, finish)
        for code in ORDER:
            kind, q, more = code // 1000, code // 10 % 100, code % 10
            if kind in (4, 5, 7, 8, 10):
                phases[kind](q, more // 2, more % 2)
            elif kind in (6, 11):
                phases[kind](q, more)
            else:
                phases[kind](q)

        for q in range(steps):
            sent = xs[q].at[pl.ds(0, 15)]
            copy(sent, sent, ag_send.at[q], xl_sem.at[q], sib).wait_send()
            for unit in range(13):
                copy(outs[q][unit], ins[q][unit], rs_send.at[q, unit], rs_recv.at[q, unit], xh_to).wait_send()
        copy(deg_all.at[pl.ds(0, rows_n - 1)], deg_all.at[pl.ds(0, rows_n - 1)], dg_send, dg_recv.at[0], rows_to[0]).wait_send()

    return kernel


def solution(mesh):
    rows_n, cols_n = mesh.shape["row"], mesh.shape["col"]

    def on_device(affinity, block_rows, block_cols, block_count, labels, labelled):
        slots, bs = affinity.shape[2], affinity.shape[3]
        steps = SWEEPS * len(WIDTHS)
        each = WIDTHS * SWEEPS
        dma = pltpu.SemaphoreType.DMA
        scratch = [
            pltpu.VMEM((slots, bs, bs), jnp.bfloat16),
            pltpu.VMEM((slots + 1, bs, max(WIDTHS)), jnp.float32),
            pltpu.VMEM((slots + 1, 8, bs), jnp.float32),
            pltpu.VMEM((rows_n, rows_n, bs), jnp.float32),
            pltpu.VMEM((rows_n, bs, 128), jnp.float32),
            pltpu.VMEM((bs, 128), jnp.float32),
            pltpu.SMEM((slots,), jnp.int32),
            pltpu.SMEM((rows_n,), jnp.int32),
            *[pltpu.VMEM((cols_n, bs, width), jnp.bfloat16) for width in each],
            *[pltpu.VMEM((4 * bs, width), jnp.float32) for width in each],
            *[pltpu.VMEM((rows, width), jnp.int16) for width in each for rows in 2 * ([bs // 2] * 12 + [bs])],
            dma,
            dma((steps,)),
            dma((steps, 2, 2)),
            dma((steps, 2, 2)),
            dma((steps, 10)),
            dma((steps,)),
            dma((steps, 13)),
            dma((steps, 13)),
            dma((rows_n - 1,)),
            dma,
        ]
        smem = pl.BlockSpec(memory_space=pltpu.SMEM)
        vmem = pl.BlockSpec(memory_space=pltpu.VMEM)
        return pl.pallas_call(
            make_kernel((slots, bs, rows_n, cols_n)),
            out_shape=jax.ShapeDtypeStruct(labels.shape, jnp.float32),
            in_specs=[smem, smem, smem, pl.BlockSpec(memory_space=pl.ANY), vmem, vmem],
            out_specs=vmem,
            scratch_shapes=scratch,
            compiler_params=pltpu.CompilerParams(
                collective_id=0, has_side_effects=True, vmem_limit_bytes=60 * 1024 * 1024
            ),
        )(block_rows, block_cols, block_count, affinity, labels, labelled.reshape(1, bs))

    placed = (
        P("row", "col", None, None, None),
        P("row", "col", None),
        P("row", "col", None),
        P("row", "col"),
        P(("row", "col"), None),
        P(("row", "col")),
    )
    return jax.shard_map(
        on_device, mesh=mesh, in_specs=placed, out_specs=P(("row", "col"), None), check_vma=False
    )
```

```python
import jax
import jax.numpy as jnp
from jax import lax
from jax.experimental import pallas as pl
from jax.experimental.pallas import tpu as pltpu
from jax.sharding import PartitionSpec as P

MESH = pl.DeviceIdType.MESH
SWEEPS = 2
WIDTHS = (256, 256, 256, 256)
PIECES = 2
UNROLL = 8
SPREAD = 0.8

ORDER = (
    2000, 2010, 0, 3000, 1000, 13011, 4001, 4011, 13010, 4000, 4002, 4003, 4010, 13001, 13000, 5001, 3010,
    13003, 5000, 5002, 13002, 5003, 2020, 6000, 6001, 7002, 7000, 5011, 4012, 5010, 4013, 13013, 7001, 8002,
    9000, 8000, 7003, 13012, 3020, 4020, 4021, 10002, 5012, 10000, 5013, 2030, 13020, 8001, 8003, 10001, 6010,
    10003, 6011, 7010, 7012, 11000, 7011, 7013, 4022, 13021, 4023, 5021, 13023, 5020, 11001, 3030, 8012,
    13030, 9010, 8010, 13022, 10012, 10010, 5022, 4031, 4030, 5023, 8013, 10013, 8011, 10011, 12000, 2040,
    6020, 6021, 7020, 7022, 11010, 7023, 4033, 7021, 4032, 5030, 9020, 13031, 4041, 4040, 13040, 8020, 8022,
    3040, 10020, 11011, 5031, 10022, 5032, 5033, 8021, 13033, 13032, 10023, 10021, 8023, 12010, 2050, 6030,
    6031, 7030, 7032, 11020, 4043, 4042, 7031, 13043, 13041, 13042, 7033, 9030, 5041, 8031, 8032, 3050, 10032,
    8030, 5040, 13051, 5042, 10030, 8033, 4051, 4050, 11021, 5043, 10031, 10033, 12020, 2060, 6040, 6041,
    7040, 4052, 7043, 4053, 13052, 11030, 5050, 8042, 8041, 7041, 13053, 3060, 9040, 5051, 4060, 13050, 7042,
    5052, 5053, 8040, 4061, 11031, 10043, 10040, 8043, 6050, 12030, 2070, 10041, 10042, 6051, 7050, 5060,
    13060, 7053, 13063, 4063, 4062, 13062, 5061, 7051, 9050, 7052, 8051, 11040, 3070, 8052, 4071, 10053,
    13061, 4070, 5062, 5063, 10050, 8053, 8050, 10051, 10052, 6060, 4072, 6061, 7060, 4073, 7062, 9060, 5070,
    8060, 7063, 13073, 5071, 13070, 13072, 8061, 7061, 13071, 8063, 5072, 5073, 8062, 10062, 10060, 6070,
    6071, 7072, 7070, 9070, 11050, 8071, 7073, 8070, 8072, 10070, 10072, 11041, 11060, 12040, 7071, 11051,
    12050, 10063, 10061, 11070, 8073, 10073, 10071, 11061, 12060, 11071, 12070,
)

PER_NAT = 2048.0 / 0.6931471805599453
ONE_CODE = 32700.0
LEAST = -32768.0


def encode(v):
    code = jnp.log(jnp.maximum(v, 1e-30)) * PER_NAT + ONE_CODE
    code = jnp.minimum(jnp.maximum(code, LEAST), 32767.0)
    return jnp.floor(code + 0.5).astype(jnp.int32).astype(jnp.int16)


def decode(q):
    code = q.astype(jnp.int32).astype(jnp.float32)
    v = jnp.exp((code - ONE_CODE) * (1.0 / PER_NAT))
    return jnp.where(code > LEAST, v, 0.0)


def make_kernel(sizes):
    slots, bs, rows_n, cols_n = sizes
    chunks = len(WIDTHS)
    half = bs // 2
    steps = SWEEPS * chunks

    def kernel(rows_s, cols_s, count_s, aff, labels, marked, out, wv, sums, deg_run, deg_all, inv, mask, prev_s, last_s, *rest):
        xs = rest[:steps]
        pend = rest[steps : 2 * steps]
        outs = [rest[2 * steps + 26 * q : 2 * steps + 26 * q + 13] for q in range(steps)]
        ins = [rest[2 * steps + 26 * q + 13 : 2 * steps + 26 * q + 26] for q in range(steps)]
        (w_sem, xl_sem, z_sem, zr_sem, sib_sem, ag_send, rs_recv, rs_send, dg_recv, dg_send) = rest[28 * steps :]

        r, c = lax.axis_index("row"), lax.axis_index("col")
        y, xh = r // 2, r % 2
        xl, z, core = c // 8, (c // 2) % 4, c % 2
        zs = [(z + k) % 4 for k in range(4)]
        ys = [(y + k) % 4 for k in range(4)]
        col_of = lambda a, b, k: a * 8 + b * 2 + k
        sib = (r, col_of(xl, z, 1 - core))
        far_xl = (r, col_of(1 - xl, z, core))
        z_to = ((r, col_of(xl, zs[1], core)), (r, col_of(xl, zs[3], core)))
        y_to = ((ys[1] * 2 + xh, c), (ys[3] * 2 + xh, c))
        xh_to = (y * 2 + 1 - xh, c)
        sides = (1 - xh, xh)
        rows_to = [((r + k) % rows_n, c) for k in range(1, rows_n)]

        barrier = pltpu.get_barrier_semaphore()
        met = [sib, far_xl, *z_to, *rows_to]
        for device in met:
            pl.semaphore_signal(barrier, inc=1, device_id=device, device_id_type=MESH)
        load = pltpu.make_async_copy(aff.at[0, 0], wv, w_sem)
        load.start()
        pl.semaphore_wait(barrier, len(met))

        def width(q):
            return WIDTHS[q % chunks]

        def lanes(q):
            return pl.ds(sum(WIDTHS[: q % chunks]), width(q))

        def copy(src, dst, send, recv, device):
            return pltpu.make_async_remote_copy(
                src_ref=src, dst_ref=dst, send_sem=send, recv_sem=recv, device_id=device, device_id_type=MESH
            )

        def put(q, ref, recv, device):
            copy(ref, ref, ag_send.at[q], recv, device).start()

        def got(q, ref, recv, device):
            copy(ref, ref, ag_send.at[q], recv, device).wait_recv()

        def own(q):
            if q < chunks:
                for h in (0, 1):
                    at = pl.ds(h * half, half)
                    xs[q][c, at, :] = labels[at, lanes(q)].astype(jnp.bfloat16)
            block = xs[q].at[c]
            put(q, block, xl_sem.at[q], far_xl)
            along_z(q, c, 0)
            put(q, block, sib_sem.at[q, 0], sib)

        def pair(q):
            b = col_of(1 - xl, z, core)
            block = xs[q].at[b]
            got(q, block, xl_sem.at[q], far_xl)
            along_z(q, b, 1)
            put(q, block, sib_sem.at[q, 1], sib)

        def along_z(q, b, kind):
            for later in (0, 1):
                for d in (0, 1):
                    part = xs[q].at[b, pl.ds(half * (1 - d if later else d), half)]
                    put(q, part, z_sem.at[q, kind, 2 * d + later], z_to[d])

        def near(q, kind, d):
            b = col_of(xl if kind == 0 else 1 - xl, zs[3] if d == 0 else zs[1], core)
            part = xs[q].at[b, pl.ds(half * d, half)]
            got(q, part, z_sem.at[q, kind, 2 * d], z_to[d])
            put(q, part, zr_sem.at[q, kind, d], z_to[d])
            put(q, part, sib_sem.at[q, 2 + 2 * kind + d], sib)

        def near_rest(q, kind, d):
            b = col_of(xl if kind == 0 else 1 - xl, zs[3] if d == 0 else zs[1], core)
            part = xs[q].at[b, pl.ds(half * (1 - d), half)]
            got(q, part, z_sem.at[q, kind, 2 * d + 1], z_to[d])
            put(q, part, sib_sem.at[q, 10 + 2 * kind + d], sib)

        def far(q, kind, d):
            b = col_of(xl if kind == 0 else 1 - xl, zs[2], core)
            part = xs[q].at[b, pl.ds(half * d, half)]
            got(q, part, zr_sem.at[q, kind, d], z_to[d])
            put(q, part, sib_sem.at[q, 6 + 2 * kind + d], sib)

        def from_sibling(q):
            for kind in (0, 1):
                side = xl if kind == 0 else 1 - xl
                got(q, xs[q].at[col_of(side, z, 1 - core)], sib_sem.at[q, kind], sib)
                for d in (0, 1):
                    b = col_of(side, zs[3] if d == 0 else zs[1], 1 - core)
                    got(q, xs[q].at[b, pl.ds(half * d, half)], sib_sem.at[q, 2 + 2 * kind + d], sib)
                    got(q, xs[q].at[b, pl.ds(half * (1 - d), half)], sib_sem.at[q, 10 + 2 * kind + d], sib)
                    part = xs[q].at[col_of(side, zs[2], 1 - core), pl.ds(half * d, half)]
                    got(q, part, sib_sem.at[q, 6 + 2 * kind + d], sib)

        def prod(q, piece):
            if piece == 0:
                from_sibling(q)
            wide = pl.ds(0, width(q))
            first = piece * (slots // PIECES)

            def several(i, _):
                for k in range(UNROLL):
                    s = first + i * UNROLL + k
                    block = xs[q][cols_s[0, 0, s]]
                    sums[s + 1, :, wide] = sums[prev_s[s], :, wide] + jnp.dot(wv[s], block, preferred_element_type=jnp.float32)
                return 0

            lax.fori_loop(0, slots // PIECES // UNROLL, several, 0)

        def share(q, rho, h):
            at = pl.ds(h * half, half)
            scale = jnp.concatenate([inv[rho, at, :]] * (width(q) // 128), axis=1)
            return sums[last_s[rho], at, pl.ds(0, width(q))] * scale

        def send_unit(q, unit, device):
            copy(outs[q][unit], ins[q][unit], rs_send.at[q, unit], rs_recv.at[q, unit], device).start()

        def got_unit(q, unit, device):
            copy(outs[q][unit], ins[q][unit], rs_send.at[q, unit], rs_recv.at[q, unit], device).wait_recv()

        def next_y(d, o):
            return (ys[1] if d == 0 else ys[3]) * 2 + sides[o]

        def send_far(q, h, o):
            unit = 2 * h + o
            outs[q][unit][...] = encode(share(q, ys[2] * 2 + sides[o], h))
            send_unit(q, unit, y_to[h])

        def send_near(q, d, o):
            unit = 4 + 4 * d + 2 * (1 - d) + o
            outs[q][unit][...] = encode(share(q, next_y(d, o), 1 - d))
            send_unit(q, unit, y_to[d])

        def set_aside(q):
            for o in (0, 1):
                for d in (0, 1):
                    pend[q][pl.ds((2 * d + o) * half, half), :] = share(q, next_y(d, o), d)
                for h in (0, 1):
                    pend[q][pl.ds((4 + 2 * o + h) * half, half), :] = share(q, y * 2 + sides[o], h)

        def relay_on(q, d, o):
            unit = 4 + 4 * d + 2 * d + o
            got_unit(q, 2 * d + o, y_to[d])
            value = pend[q][pl.ds((2 * d + o) * half, half), :] + decode(ins[q][2 * d + o][...])
            outs[q][unit][...] = encode(value)
            send_unit(q, unit, y_to[d])

        def over_y(q, o):
            for h in (0, 1):
                for d in (0, 1):
                    got_unit(q, 4 + 4 * d + 2 * h + o, y_to[d])
            for h in (0, 1):
                at = pl.ds((4 + 2 * o + h) * half, half)
                value = pend[q][at, :] + decode(ins[q][4 + 2 * h + o][...]) + decode(ins[q][8 + 2 * h + o][...])
                if o == 0:
                    outs[q][12][pl.ds(h * half, half), :] = encode(value)
                else:
                    pend[q][at, :] = value
            if o == 0:
                send_unit(q, 12, xh_to)

        def finish(q):
            got_unit(q, 12, xh_to)
            for h in (0, 1):
                at = pl.ds(h * half, half)
                total = pend[q][pl.ds((6 + h) * half, half), :] + decode(ins[q][12][at, :])
                prior = labels[at, lanes(q)]
                keep = jnp.concatenate([mask[at, :]] * (width(q) // 128), axis=1)
                value = jnp.where(keep == 1.0, prior, SPREAD * total + (1.0 - SPREAD) * prior)
                if q < steps - chunks:
                    xs[q + chunks][c, at, :] = value.astype(jnp.bfloat16)
                else:
                    out[at, lanes(q)] = value

        def degrees_out(q):
            live = count_s[0, 0]

            def chain(s, lasts):
                row = rows_s[0, 0, s]
                before = jnp.int32(0)
                new = []
                for rho in range(rows_n):
                    before = jnp.where(row == rho, lasts[rho], before)
                    new.append(jnp.where((row == rho) & (s < live), s + 1, lasts[rho]))
                prev_s[s] = before
                return tuple(new)

            lasts = lax.fori_loop(0, slots, chain, (jnp.int32(0),) * rows_n)
            for rho in range(rows_n):
                last_s[rho] = lasts[rho]
            sums[0] = jnp.zeros((bs, max(WIDTHS)), jnp.float32)
            deg_run[0] = jnp.zeros((8, bs), jnp.float32)
            load.wait()

            def row_sums(i, _):
                ones = jnp.ones((8, bs), jnp.bfloat16)
                for k in range(4):
                    s = i * 4 + k
                    part = lax.dot_general(ones, wv[s], (((1,), (1,)), ((), ())), preferred_element_type=jnp.float32)
                    deg_run[s + 1] = deg_run[prev_s[s]] + part
                return 0

            lax.fori_loop(0, slots // 4, row_sums, 0)
            for rho in range(rows_n):
                deg_all[r, pl.ds(rho, 1), :] = deg_run[last_s[rho], pl.ds(0, 1), :]
            for k, device in enumerate(rows_to):
                copy(deg_all.at[r], deg_all.at[r], dg_send, dg_recv.at[k], device).start()

        def degrees_in(q):
            for k in range(1, rows_n):
                block = deg_all.at[(r + rows_n - k) % rows_n]
                copy(block, block, dg_send, dg_recv.at[k - 1], rows_to[k - 1]).wait_recv()
            degree = deg_all[0]
            for k in range(1, rows_n):
                degree = degree + deg_all[k]
            marks = jnp.broadcast_to(marked[...].astype(jnp.float32), (8, bs))
            stack = jnp.concatenate([1.0 / degree, marks, jnp.zeros((112, bs), jnp.float32)], axis=0)
            turned = jnp.transpose(stack)
            for rho in range(rows_n):
                inv[rho] = jnp.broadcast_to(turned[:, rho : rho + 1], (bs, 128))
            mask[...] = jnp.broadcast_to(turned[:, rows_n : rows_n + 1], (bs, 128))

        phases = (degrees_out, degrees_in, own, pair, near, far, prod, send_far, send_near, set_aside, relay_on, over_y, finish,
                  near_rest)
        for code in ORDER:
            kind, q, more = code // 1000, code // 10 % 100, code % 10
            if kind in (4, 5, 7, 8, 10, 13):
                phases[kind](q, more // 2, more % 2)
            elif kind in (6, 11):
                phases[kind](q, more)
            else:
                phases[kind](q)

        for q in range(steps):
            sent = xs[q].at[pl.ds(0, 15)]
            copy(sent, sent, ag_send.at[q], xl_sem.at[q], sib).wait_send()
            for unit in range(13):
                copy(outs[q][unit], ins[q][unit], rs_send.at[q, unit], rs_recv.at[q, unit], xh_to).wait_send()
        copy(deg_all.at[pl.ds(0, rows_n - 1)], deg_all.at[pl.ds(0, rows_n - 1)], dg_send, dg_recv.at[0], rows_to[0]).wait_send()

    return kernel


def solution(mesh):
    rows_n, cols_n = mesh.shape["row"], mesh.shape["col"]

    def on_device(affinity, block_rows, block_cols, block_count, labels, labelled):
        slots, bs = affinity.shape[2], affinity.shape[3]
        steps = SWEEPS * len(WIDTHS)
        each = WIDTHS * SWEEPS
        dma = pltpu.SemaphoreType.DMA
        scratch = [
            pltpu.VMEM((slots, bs, bs), jnp.bfloat16),
            pltpu.VMEM((slots + 1, bs, max(WIDTHS)), jnp.float32),
            pltpu.VMEM((slots + 1, 8, bs), jnp.float32),
            pltpu.VMEM((rows_n, rows_n, bs), jnp.float32),
            pltpu.VMEM((rows_n, bs, 128), jnp.float32),
            pltpu.VMEM((bs, 128), jnp.float32),
            pltpu.SMEM((slots,), jnp.int32),
            pltpu.SMEM((rows_n,), jnp.int32),
            *[pltpu.VMEM((cols_n, bs, width), jnp.bfloat16) for width in each],
            *[pltpu.VMEM((4 * bs, width), jnp.float32) for width in each],
            *[pltpu.VMEM((rows, width), jnp.int16) for width in each for rows in 2 * ([bs // 2] * 12 + [bs])],
            dma,
            dma((steps,)),
            dma((steps, 2, 4)),
            dma((steps, 2, 2)),
            dma((steps, 14)),
            dma((steps,)),
            dma((steps, 13)),
            dma((steps, 13)),
            dma((rows_n - 1,)),
            dma,
        ]
        smem = pl.BlockSpec(memory_space=pltpu.SMEM)
        vmem = pl.BlockSpec(memory_space=pltpu.VMEM)
        return pl.pallas_call(
            make_kernel((slots, bs, rows_n, cols_n)),
            out_shape=jax.ShapeDtypeStruct(labels.shape, jnp.float32),
            in_specs=[smem, smem, smem, pl.BlockSpec(memory_space=pl.ANY), vmem, vmem],
            out_specs=vmem,
            scratch_shapes=scratch,
            compiler_params=pltpu.CompilerParams(
                collective_id=0, has_side_effects=True, vmem_limit_bytes=60 * 1024 * 1024
            ),
        )(block_rows, block_cols, block_count, affinity, labels, labelled.reshape(1, bs))

    placed = (
        P("row", "col", None, None, None),
        P("row", "col", None),
        P("row", "col", None),
        P("row", "col"),
        P(("row", "col"), None),
        P(("row", "col")),
    )
    return jax.shard_map(
        on_device, mesh=mesh, in_specs=placed, out_specs=P(("row", "col"), None), check_vma=False
    )
```

```python
import jax
import jax.numpy as jnp
from jax import lax
from jax.experimental import pallas as pl
from jax.experimental.pallas import tpu as pltpu
from jax.sharding import PartitionSpec as P

MESH = pl.DeviceIdType.MESH
SWEEPS = 2
WIDTHS = (256, 256, 256, 256)
PIECES = 2
UNROLL = 8
SPREAD = 0.8

ORDER = (
    2000, 0, 2010, 3000, 4001, 4000, 4011, 4002, 4003, 1000, 5001, 5000, 3010, 5011, 5002, 5003, 4010, 2020,
    6000, 6001, 7000, 7002, 4013, 4012, 5010, 7001, 7003, 3020, 8000, 9000, 2030, 8002, 5013, 10000, 10002,
    8001, 5012, 10003, 8003, 4021, 10001, 6010, 4020, 6011, 7010, 7012, 11000, 4023, 4022, 7011, 7013, 11001,
    3030, 8010, 9010, 8012, 5023, 10012, 5021, 10010, 4030, 5022, 4031, 8013, 8011, 5020, 10011, 10013, 12000,
    2040, 6020, 6021, 7020, 7022, 11010, 4033, 7021, 7023, 5031, 4032, 3040, 8020, 11011, 8022, 4040, 9020,
    4041, 10022, 10020, 5033, 5030, 5032, 8023, 8021, 10023, 10021, 12010, 2050, 6030, 6031, 7030, 7032,
    11020, 4043, 5040, 7031, 4042, 7033, 5041, 3050, 9030, 8030, 8032, 4051, 10030, 10032, 11021, 4050, 8031,
    10031, 8033, 10033, 5043, 5042, 12020, 2060, 6040, 6041, 7043, 7040, 5050, 4053, 4052, 11030, 7042, 8040,
    3060, 7041, 9040, 8043, 8042, 4061, 11031, 5053, 5051, 5052, 10040, 8041, 4060, 10043, 10042, 6050, 12030,
    2070, 10041, 6051, 7051, 7053, 4062, 9050, 4063, 7052, 5060, 7050, 11040, 8051, 8053, 3070, 10051, 8050,
    5061, 10053, 5063, 5062, 8052, 10050, 4070, 4071, 10052, 6060, 6061, 4072, 4073, 7060, 7062, 5071, 5070,
    9060, 8062, 8061, 8063, 7061, 7063, 5072, 5073, 10060, 8060, 10062, 6070, 6071, 7070, 7072, 11050, 9070,
    8071, 8070, 7073, 8072, 10072, 10070, 11041, 11060, 12040, 11051, 7071, 12050, 10073, 10063, 10061, 11070,
    8073, 10071, 11061, 11071, 12060, 12070,
)

PER_NAT = 2048.0 / 0.6931471805599453
ONE_CODE = 32700.0
LEAST = -32768.0


def encode(v):
    code = jnp.log(jnp.maximum(v, 1e-30)) * PER_NAT + ONE_CODE
    code = jnp.minimum(jnp.maximum(code, LEAST), 32767.0)
    return jnp.floor(code + 0.5).astype(jnp.int32).astype(jnp.int16)


def decode(q):
    code = q.astype(jnp.int32).astype(jnp.float32)
    v = jnp.exp((code - ONE_CODE) * (1.0 / PER_NAT))
    return jnp.where(code > LEAST, v, 0.0)


def make_kernel(sizes):
    slots, bs, rows_n, cols_n = sizes
    chunks = len(WIDTHS)
    half = bs // 2
    steps = SWEEPS * chunks

    def kernel(rows_s, cols_s, count_s, aff, labels, marked, out, wv, sums, deg_run, deg_all, inv, mask, prev_s, last_s, *rest):
        xs = rest[:steps]
        pend = rest[steps : 2 * steps]
        outs = [rest[2 * steps + 26 * q : 2 * steps + 26 * q + 13] for q in range(steps)]
        ins = [rest[2 * steps + 26 * q + 13 : 2 * steps + 26 * q + 26] for q in range(steps)]
        (w_sem, xl_sem, z_sem, zr_sem, sib_sem, ag_send, rs_recv, rs_send, dg_recv, dg_send) = rest[28 * steps :]

        r, c = lax.axis_index("row"), lax.axis_index("col")
        y, xh = r // 2, r % 2
        xl, z, core = c // 8, (c // 2) % 4, c % 2
        zs = [(z + k) % 4 for k in range(4)]
        ys = [(y + k) % 4 for k in range(4)]
        col_of = lambda a, b, k: a * 8 + b * 2 + k
        sib = (r, col_of(xl, z, 1 - core))
        far_xl = (r, col_of(1 - xl, z, core))
        z_to = ((r, col_of(xl, zs[1], core)), (r, col_of(xl, zs[3], core)))
        y_to = ((ys[1] * 2 + xh, c), (ys[3] * 2 + xh, c))
        xh_to = (y * 2 + 1 - xh, c)
        sides = (1 - xh, xh)
        rows_to = [((r + k) % rows_n, c) for k in range(1, rows_n)]

        barrier = pltpu.get_barrier_semaphore()
        met = [sib, far_xl, *z_to, *rows_to]
        for device in met:
            pl.semaphore_signal(barrier, inc=1, device_id=device, device_id_type=MESH)
        load = pltpu.make_async_copy(aff.at[0, 0], wv, w_sem)
        load.start()
        pl.semaphore_wait(barrier, len(met))

        def width(q):
            return WIDTHS[q % chunks]

        def lanes(q):
            return pl.ds(sum(WIDTHS[: q % chunks]), width(q))

        def copy(src, dst, send, recv, device):
            return pltpu.make_async_remote_copy(
                src_ref=src, dst_ref=dst, send_sem=send, recv_sem=recv, device_id=device, device_id_type=MESH
            )

        def put(q, ref, recv, device):
            copy(ref, ref, ag_send.at[q], recv, device).start()

        def got(q, ref, recv, device):
            copy(ref, ref, ag_send.at[q], recv, device).wait_recv()

        def own(q):
            if q < chunks:
                for h in (0, 1):
                    at = pl.ds(h * half, half)
                    xs[q][c, at, :] = labels[at, lanes(q)].astype(jnp.bfloat16)
            block = xs[q].at[c]
            put(q, block, xl_sem.at[q], far_xl)
            put(q, block, z_sem.at[q, 0, 0], z_to[0])
            put(q, block, z_sem.at[q, 0, 1], z_to[1])
            put(q, block, sib_sem.at[q, 0], sib)

        def pair(q):
            block = xs[q].at[col_of(1 - xl, z, core)]
            got(q, block, xl_sem.at[q], far_xl)
            put(q, block, z_sem.at[q, 1, 0], z_to[0])
            put(q, block, z_sem.at[q, 1, 1], z_to[1])
            put(q, block, sib_sem.at[q, 1], sib)

        def near(q, kind, d):
            b = col_of(xl if kind == 0 else 1 - xl, zs[3] if d == 0 else zs[1], core)
            got(q, xs[q].at[b], z_sem.at[q, kind, d], z_to[d])
            put(q, xs[q].at[b, pl.ds(half * d, half)], zr_sem.at[q, kind, d], z_to[d])
            put(q, xs[q].at[b], sib_sem.at[q, 2 + 2 * kind + d], sib)

        def far(q, kind, d):
            b = col_of(xl if kind == 0 else 1 - xl, zs[2], core)
            part = xs[q].at[b, pl.ds(half * d, half)]
            got(q, part, zr_sem.at[q, kind, d], z_to[d])
            put(q, part, sib_sem.at[q, 6 + 2 * kind + d], sib)

        def from_sibling(q):
            for kind in (0, 1):
                side = xl if kind == 0 else 1 - xl
                got(q, xs[q].at[col_of(side, z, 1 - core)], sib_sem.at[q, kind], sib)
                for d in (0, 1):
                    block = xs[q].at[col_of(side, zs[3] if d == 0 else zs[1], 1 - core)]
                    got(q, block, sib_sem.at[q, 2 + 2 * kind + d], sib)
                    part = xs[q].at[col_of(side, zs[2], 1 - core), pl.ds(half * d, half)]
                    got(q, part, sib_sem.at[q, 6 + 2 * kind + d], sib)

        def prod(q, piece):
            if piece == 0:
                from_sibling(q)
            wide = pl.ds(0, width(q))
            first = piece * (slots // PIECES)

            def several(i, _):
                for k in range(UNROLL):
                    s = first + i * UNROLL + k
                    block = xs[q][cols_s[0, 0, s]]
                    sums[s + 1, :, wide] = sums[prev_s[s], :, wide] + jnp.dot(wv[s], block, preferred_element_type=jnp.float32)
                return 0

            lax.fori_loop(0, slots // PIECES // UNROLL, several, 0)

        def share(q, rho, h):
            at = pl.ds(h * half, half)
            scale = jnp.concatenate([inv[rho, at, :]] * (width(q) // 128), axis=1)
            return sums[last_s[rho], at, pl.ds(0, width(q))] * scale

        def send_unit(q, unit, device):
            copy(outs[q][unit], ins[q][unit], rs_send.at[q, unit], rs_recv.at[q, unit], device).start()

        def got_unit(q, unit, device):
            copy(outs[q][unit], ins[q][unit], rs_send.at[q, unit], rs_recv.at[q, unit], device).wait_recv()

        def next_y(d, o):
            return (ys[1] if d == 0 else ys[3]) * 2 + sides[o]

        def send_far(q, h, o):
            unit = 2 * h + o
            outs[q][unit][...] = encode(share(q, ys[2] * 2 + sides[o], h))
            send_unit(q, unit, y_to[h])

        def send_near(q, d, o):
            unit = 4 + 4 * d + 2 * (1 - d) + o
            outs[q][unit][...] = encode(share(q, next_y(d, o), 1 - d))
            send_unit(q, unit, y_to[d])

        def set_aside(q):
            for o in (0, 1):
                for d in (0, 1):
                    pend[q][pl.ds((2 * d + o) * half, half), :] = share(q, next_y(d, o), d)
                for h in (0, 1):
                    pend[q][pl.ds((4 + 2 * o + h) * half, half), :] = share(q, y * 2 + sides[o], h)

        def relay_on(q, d, o):
            unit = 4 + 4 * d + 2 * d + o
            got_unit(q, 2 * d + o, y_to[d])
            value = pend[q][pl.ds((2 * d + o) * half, half), :] + decode(ins[q][2 * d + o][...])
            outs[q][unit][...] = encode(value)
            send_unit(q, unit, y_to[d])

        def over_y(q, o):
            for h in (0, 1):
                for d in (0, 1):
                    got_unit(q, 4 + 4 * d + 2 * h + o, y_to[d])
            for h in (0, 1):
                at = pl.ds((4 + 2 * o + h) * half, half)
                value = pend[q][at, :] + decode(ins[q][4 + 2 * h + o][...]) + decode(ins[q][8 + 2 * h + o][...])
                if o == 0:
                    outs[q][12][pl.ds(h * half, half), :] = encode(value)
                else:
                    pend[q][at, :] = value
            if o == 0:
                send_unit(q, 12, xh_to)

        def finish(q):
            got_unit(q, 12, xh_to)
            for h in (0, 1):
                at = pl.ds(h * half, half)
                total = pend[q][pl.ds((6 + h) * half, half), :] + decode(ins[q][12][at, :])
                prior = labels[at, lanes(q)]
                keep = jnp.concatenate([mask[at, :]] * (width(q) // 128), axis=1)
                value = jnp.where(keep == 1.0, prior, SPREAD * total + (1.0 - SPREAD) * prior)
                if q < steps - chunks:
                    xs[q + chunks][c, at, :] = value.astype(jnp.bfloat16)
                else:
                    out[at, lanes(q)] = value

        def degrees_out(q):
            live = count_s[0, 0]

            def chain(s, lasts):
                row = rows_s[0, 0, s]
                before = jnp.int32(0)
                new = []
                for rho in range(rows_n):
                    before = jnp.where(row == rho, lasts[rho], before)
                    new.append(jnp.where((row == rho) & (s < live), s + 1, lasts[rho]))
                prev_s[s] = before
                return tuple(new)

            lasts = lax.fori_loop(0, slots, chain, (jnp.int32(0),) * rows_n)
            for rho in range(rows_n):
                last_s[rho] = lasts[rho]
            sums[0] = jnp.zeros((bs, max(WIDTHS)), jnp.float32)
            deg_run[0] = jnp.zeros((8, bs), jnp.float32)
            load.wait()

            def row_sums(i, _):
                ones = jnp.ones((8, bs), jnp.bfloat16)
                for k in range(4):
                    s = i * 4 + k
                    part = lax.dot_general(ones, wv[s], (((1,), (1,)), ((), ())), preferred_element_type=jnp.float32)
                    deg_run[s + 1] = deg_run[prev_s[s]] + part
                return 0

            lax.fori_loop(0, slots // 4, row_sums, 0)
            for rho in range(rows_n):
                deg_all[r, pl.ds(rho, 1), :] = deg_run[last_s[rho], pl.ds(0, 1), :]
            for k, device in enumerate(rows_to):
                copy(deg_all.at[r], deg_all.at[r], dg_send, dg_recv.at[k], device).start()

        def degrees_in(q):
            for k in range(1, rows_n):
                block = deg_all.at[(r + rows_n - k) % rows_n]
                copy(block, block, dg_send, dg_recv.at[k - 1], rows_to[k - 1]).wait_recv()
            degree = deg_all[0]
            for k in range(1, rows_n):
                degree = degree + deg_all[k]
            marks = jnp.broadcast_to(marked[...].astype(jnp.float32), (8, bs))
            stack = jnp.concatenate([1.0 / degree, marks, jnp.zeros((112, bs), jnp.float32)], axis=0)
            turned = jnp.transpose(stack)
            for rho in range(rows_n):
                inv[rho] = jnp.broadcast_to(turned[:, rho : rho + 1], (bs, 128))
            mask[...] = jnp.broadcast_to(turned[:, rows_n : rows_n + 1], (bs, 128))

        phases = (degrees_out, degrees_in, own, pair, near, far, prod, send_far, send_near, set_aside, relay_on, over_y, finish)
        for code in ORDER:
            kind, q, more = code // 1000, code // 10 % 100, code % 10
            if kind in (4, 5, 7, 8, 10):
                phases[kind](q, more // 2, more % 2)
            elif kind in (6, 11):
                phases[kind](q, more)
            else:
                phases[kind](q)

        for q in range(steps):
            sent = xs[q].at[pl.ds(0, 15)]
            copy(sent, sent, ag_send.at[q], xl_sem.at[q], sib).wait_send()
            for unit in range(13):
                copy(outs[q][unit], ins[q][unit], rs_send.at[q, unit], rs_recv.at[q, unit], xh_to).wait_send()
        copy(deg_all.at[pl.ds(0, rows_n - 1)], deg_all.at[pl.ds(0, rows_n - 1)], dg_send, dg_recv.at[0], rows_to[0]).wait_send()

    return kernel


def solution(mesh):
    rows_n, cols_n = mesh.shape["row"], mesh.shape["col"]

    def on_device(affinity, block_rows, block_cols, block_count, labels, labelled):
        slots, bs = affinity.shape[2], affinity.shape[3]
        steps = SWEEPS * len(WIDTHS)
        each = WIDTHS * SWEEPS
        dma = pltpu.SemaphoreType.DMA
        scratch = [
            pltpu.VMEM((slots, bs, bs), jnp.bfloat16),
            pltpu.VMEM((slots + 1, bs, max(WIDTHS)), jnp.float32),
            pltpu.VMEM((slots + 1, 8, bs), jnp.float32),
            pltpu.VMEM((rows_n, rows_n, bs), jnp.float32),
            pltpu.VMEM((rows_n, bs, 128), jnp.float32),
            pltpu.VMEM((bs, 128), jnp.float32),
            pltpu.SMEM((slots,), jnp.int32),
            pltpu.SMEM((rows_n,), jnp.int32),
            *[pltpu.VMEM((cols_n, bs, width), jnp.bfloat16) for width in each],
            *[pltpu.VMEM((4 * bs, width), jnp.float32) for width in each],
            *[pltpu.VMEM((rows, width), jnp.int16) for width in each for rows in 2 * ([bs // 2] * 12 + [bs])],
            dma,
            dma((steps,)),
            dma((steps, 2, 2)),
            dma((steps, 2, 2)),
            dma((steps, 10)),
            dma((steps,)),
            dma((steps, 13)),
            dma((steps, 13)),
            dma((rows_n - 1,)),
            dma,
        ]
        smem = pl.BlockSpec(memory_space=pltpu.SMEM)
        vmem = pl.BlockSpec(memory_space=pltpu.VMEM)
        return pl.pallas_call(
            make_kernel((slots, bs, rows_n, cols_n)),
            out_shape=jax.ShapeDtypeStruct(labels.shape, jnp.float32),
            in_specs=[smem, smem, smem, pl.BlockSpec(memory_space=pl.ANY), vmem, vmem],
            out_specs=vmem,
            scratch_shapes=scratch,
            compiler_params=pltpu.CompilerParams(
                collective_id=0, has_side_effects=True, vmem_limit_bytes=60 * 1024 * 1024
            ),
        )(block_rows, block_cols, block_count, affinity, labels, labelled.reshape(1, bs))

    placed = (
        P("row", "col", None, None, None),
        P("row", "col", None),
        P("row", "col", None),
        P("row", "col"),
        P(("row", "col"), None),
        P(("row", "col")),
    )
    return jax.shard_map(
        on_device, mesh=mesh, in_specs=placed, out_specs=P(("row", "col"), None), check_vma=False
    )
```
